32 devices in a mesh: groups: 2 (over y), row: 4 (over z), col: 2 (over x), sub: 2 (over core).
Axes of the slice: x: 2, y: 2, z: 4, core: 2. Of those that a mesh axis runs over, the one named last changes fastest.
Arguments:
- stream_in: bfloat16 [4096, 5376], P(('groups', 'row'), ('col', 'sub')), parts along dimension 0, may hold values from -6 to 6
- in_gain: float32 [5376], replicated, may hold values from 0.1 to 1.9
- query_weight: bfloat16 [5376, 4096], P('row', ('col', 'sub')), may hold values from -0.078125 to 0.078125
- key_matrix: bfloat16 [5376, 2048], P('row', ('col', 'sub')), may hold values from -0.078125 to 0.078125
- value_matrix: bfloat16 [5376, 2048], P('row', ('col', 'sub')), may hold values from -0.078125 to 0.078125
- query_gain: float32 [128], replicated, may hold values from 0.45 to 10, as said below
- key_norm_gain: float32 [128], replicated, may hold values from 0.45 to 10, as said below
- output_weight: bfloat16 [4096, 5376], P('row', ('col', 'sub')), may hold values from -3 to 3
- post_gain: float32 [5376], P(('col', 'sub')), may hold values from 0.1 to 1.9
Outputs:
- stream_out: bfloat16 [4096, 5376], P(('groups', 'row'), ('col', 'sub')), parts along dimension 0
The draws below stay inside these ranges and needn't reach their ends.
There are 2 independent parts, one for each index of `groups`. The reference program is written for one: setup_inputs(seed, part) draws one part's arguments, and reference() takes and returns one part's arrays. A program takes and returns all parts, laid end to end along the dimension named above; an argument that names none is the same for every part. Nothing has to cross between parts.
Inputs may be any that keep to these rules, and one draw needn't show every extreme that they name: `query_gain`: positive. `key_norm_gain`: positive.
All inputs are finite; a program needn't handle non-finite values.
Results may differ from the reference program's by a relative error of at most 0.014.
The reference program's roundings to bfloat16 on the way count: a program that leaves them out, or rounds other values in their place, can miss the bound.
Values may be sent and summed in bfloat16 or wider, within the bound.
A program may use at most 128 MiB of HBM per device.

```python
import jax
import jax.numpy as jnp
from jax import lax

MODEL_WIDTH = 5376
QUERY_HEAD_COUNT = 32
KEY_VALUE_HEADS = 16
HEAD_DIM = 128
WINDOW_LENGTH = 1024
TOKENS_PER_ROW = 512
S = 2048
N_ROW = 4


def head_gain(key):
    return jnp.exp(jax.random.uniform(key, (HEAD_DIM,), jnp.float32, -0.69, 0.69))


def draw_query_gain(key, part):
    return head_gain(jax.random.fold_in(key, 101))


def draw_key_norm_gain(key, part):
    return head_gain(jax.random.fold_in(key, 202))


def draw_output_weight(key, part):
    fan_rows = QUERY_HEAD_COUNT * HEAD_DIM
    base_values = jnp.clip(jax.random.normal(jax.random.fold_in(key, 1), (fan_rows, MODEL_WIDTH), jnp.float32), -6.0, 6.0)
    column = jnp.arange(MODEL_WIDTH, dtype=jnp.float32) / MODEL_WIDTH
    row_jitter = jnp.exp(jax.random.uniform(jax.random.fold_in(key, 2), (fan_rows, 1), jnp.float32, -0.5, 0.5))
    column_scale = jnp.exp(2.3 * column + jax.random.uniform(jax.random.fold_in(key, 3), (MODEL_WIDTH,), jnp.float32, -0.5, 0.5))
    return (base_values * row_jitter * column_scale[None, :] / 64.0).astype(jnp.bfloat16)


def level_of(own_key, shape, cuts, low, top_value):
    level = 1.0
    for position, parts in cuts:
        draws = jax.random.uniform(jax.random.fold_in(jax.random.fold_in(own_key, 6), position), (parts,), jnp.float32, low / len(cuts), top_value / len(cuts))
        level = level * jnp.repeat(jnp.exp(draws), shape[position] // parts).reshape((-1,) + (1,) * (len(shape) - 1 - position))
    return level


def centred(stream_key, shape, deviation, limit, pieces=(), kind=jnp.bfloat16):
    values = deviation * jax.random.normal(stream_key, shape, jnp.float32)
    if pieces:
        values = values * level_of(stream_key, shape, pieces, -0.22, 0.18)
    return jnp.clip(values, -limit, limit).astype(kind)


def setup_inputs(seed: int = 0, part: int = 0) -> dict:
    keys = jax.random.split(jax.random.key(seed), 10)
    own_keys = jax.random.split(jax.random.fold_in(keys[9], part), 10)
    stream_in = centred(own_keys[0], (S, MODEL_WIDTH), 1.0, 6.0, ((0, 4), (1, 4)))
    in_gain = jnp.clip(1.0 + 0.18 * jax.random.normal(keys[1], (MODEL_WIDTH,), jnp.float32), 0.1, 1.9)
    query_weight = centred(keys[2], (MODEL_WIDTH, QUERY_HEAD_COUNT * HEAD_DIM), MODEL_WIDTH ** -0.5, 0.078125, ((0, 4), (1, 4)))
    key_matrix = centred(keys[3], (MODEL_WIDTH, KEY_VALUE_HEADS * HEAD_DIM), MODEL_WIDTH ** -0.5, 0.078125, ((0, 4), (1, 4)))
    value_matrix = centred(keys[4], (MODEL_WIDTH, KEY_VALUE_HEADS * HEAD_DIM), MODEL_WIDTH ** -0.5, 0.078125, ((0, 4), (1, 4)))
    query_gain = draw_query_gain(jax.random.fold_in(keys[9], 71), part)
    key_norm_gain = draw_key_norm_gain(jax.random.fold_in(keys[9], 71), part)
    output_weight = draw_output_weight(jax.random.fold_in(keys[9], 71), part)
    post_gain = jnp.clip(1.0 + 0.18 * jax.random.normal(keys[8], (MODEL_WIDTH,), jnp.float32), 0.1, 1.9)
    return dict(stream_in=stream_in, in_gain=in_gain, query_weight=query_weight, key_matrix=key_matrix, value_matrix=value_matrix, query_gain=query_gain, key_norm_gain=key_norm_gain, output_weight=output_weight, post_gain=post_gain)


EPSILON = 1e-06

def root_mean_scale(values, gain):
    return values * lax.rsqrt(lax.optimization_barrier(jnp.mean(values * values, axis=-1, keepdims=True)) + EPSILON) * gain

def apply_rotary(tensor, token_positions):
    half_dim = tensor.shape[-1] // 2
    inverse = 10000.0 ** (-(jnp.arange(half_dim, dtype=jnp.float32) * 2.0) / tensor.shape[-1])
    angles = token_positions[:, None] * inverse[None, :]
    cosine = jnp.cos(angles)[:, None, :]
    sine_part = jnp.sin(angles)[:, None, :]
    first_half = tensor[..., :half_dim]
    second_half = tensor[..., half_dim:]
    return jnp.concatenate([first_half * cosine - second_half * sine_part, second_half * cosine + first_half * sine_part], axis=-1)

def reference(stream_in, in_gain, query_weight, key_matrix, value_matrix, query_gain, key_norm_gain, output_weight, post_gain):
    sequence_length = TOKENS_PER_ROW * N_ROW
    group_count = QUERY_HEAD_COUNT // KEY_VALUE_HEADS
    scale_factor = float(MODEL_WIDTH // QUERY_HEAD_COUNT) ** (-0.5)
    residual = stream_in.astype(jnp.float32)
    normed = root_mean_scale(residual, in_gain).astype(jnp.bfloat16)
    query_proj = jnp.dot(normed, query_weight, preferred_element_type=jnp.float32)
    projected_keys = jnp.dot(normed, key_matrix, preferred_element_type=jnp.float32)
    projected_values = jnp.dot(normed, value_matrix, preferred_element_type=jnp.float32).astype(jnp.bfloat16)
    token_positions = jnp.arange(sequence_length, dtype=jnp.int32).astype(jnp.float32)
    query_rot = apply_rotary(root_mean_scale(query_proj.reshape(sequence_length, QUERY_HEAD_COUNT, HEAD_DIM), query_gain), token_positions).astype(jnp.bfloat16)
    rotary_keys = apply_rotary(root_mean_scale(projected_keys.reshape(sequence_length, KEY_VALUE_HEADS, HEAD_DIM), key_norm_gain), token_positions).astype(jnp.bfloat16)
    value_head_rows = projected_values.reshape(sequence_length, KEY_VALUE_HEADS, HEAD_DIM)
    key_rows_padded = jnp.concatenate([jnp.zeros((WINDOW_LENGTH, KEY_VALUE_HEADS, HEAD_DIM), jnp.bfloat16), rotary_keys], axis=0)
    value_rows_padded = jnp.concatenate([jnp.zeros((WINDOW_LENGTH, KEY_VALUE_HEADS, HEAD_DIM), jnp.bfloat16), value_head_rows], axis=0)
    band_extent = WINDOW_LENGTH + TOKENS_PER_ROW

    def one_block(block_index):
        leading_row = (block_index * TOKENS_PER_ROW).astype(jnp.int32)
        starting_index = jnp.zeros((), jnp.int32)
        query_block_tile = lax.dynamic_slice(query_rot, (leading_row, starting_index, starting_index), (TOKENS_PER_ROW, QUERY_HEAD_COUNT, HEAD_DIM))
        query_block_tile = query_block_tile.reshape(TOKENS_PER_ROW, KEY_VALUE_HEADS, group_count, HEAD_DIM).astype(jnp.float32)
        key_block_tile = lax.dynamic_slice(key_rows_padded, (leading_row, starting_index, starting_index), (band_extent, KEY_VALUE_HEADS, HEAD_DIM)).astype(jnp.float32)
        value_block_tile = lax.dynamic_slice(value_rows_padded, (leading_row, starting_index, starting_index), (band_extent, KEY_VALUE_HEADS, HEAD_DIM)).astype(jnp.float32)
        scores = jnp.einsum('qhgd,shd->hgqs', query_block_tile, key_block_tile) * scale_factor
        query_places = leading_row + jnp.arange(TOKENS_PER_ROW, dtype=jnp.int32)
        key_places = leading_row - WINDOW_LENGTH + jnp.arange(band_extent, dtype=jnp.int32)
        distance = query_places[:, None] - key_places[None, :]
        visible = (distance >= 0) & (distance < WINDOW_LENGTH) & (key_places[None, :] >= 0)
        scores = jnp.where(visible, scores, -1e+30)
        row_max = lax.optimization_barrier(jnp.max(scores, axis=-1, keepdims=True))
        exponent = jnp.exp(scores - row_max)
        weights = (exponent / lax.optimization_barrier(jnp.sum(exponent, axis=-1, keepdims=True))).astype(jnp.bfloat16)
        attended = jnp.einsum('hgqs,shd->qhgd', weights.astype(jnp.float32), value_block_tile)
        return attended.reshape(TOKENS_PER_ROW, QUERY_HEAD_COUNT * HEAD_DIM).astype(jnp.bfloat16)
    attended = lax.map(one_block, jnp.arange(N_ROW, dtype=jnp.int32)).reshape(sequence_length, QUERY_HEAD_COUNT * HEAD_DIM)
    branch = jnp.dot(attended, output_weight, preferred_element_type=jnp.float32)
    return (residual + root_mean_scale(branch, post_gain)).astype(jnp.bfloat16)
```

```python
import jax
import jax.numpy as jnp
from jax import lax
from jax.sharding import PartitionSpec as P

MODEL_WIDTH = 5376
QUERY_HEAD_COUNT = 32
WINDOW_LENGTH = 1024


EPSILON = 1e-06


def shifted(x, axis, by):
    count = lax.axis_size(axis)
    pairs = [(i, i + by) for i in range(count) if 0 <= i + by < count]
    return lax.ppermute(x, axis, pairs)


def root_mean_scale(values, gain):
    return values * lax.rsqrt(jnp.mean(values * values, axis=-1, keepdims=True) + EPSILON) * gain


def apply_rotary(tensor, token_positions):
    half_dim = tensor.shape[-1] // 2
    inverse = 10000.0 ** (-(jnp.arange(half_dim, dtype=jnp.float32) * 2.0) / tensor.shape[-1])
    angles = token_positions[:, None] * inverse[None, :]
    cosine = jnp.cos(angles)[:, None, :]
    sine_part = jnp.sin(angles)[:, None, :]
    first_half = tensor[..., :half_dim]
    second_half = tensor[..., half_dim:]
    return jnp.concatenate(
        [
            first_half * cosine - second_half * sine_part,
            second_half * cosine + first_half * sine_part,
        ],
        axis=-1,
    )


def on_device(
    stream_in,
    in_gain,
    query_weight,
    key_matrix,
    value_matrix,
    query_gain,
    key_norm_gain,
    output_weight,
    post_gain,
):
    token_rows = lax.all_gather(stream_in, ("col", "sub"), axis=1, tiled=True)
    tokens = token_rows.shape[0]
    normed = root_mean_scale(token_rows.astype(jnp.float32), in_gain).astype(jnp.bfloat16)

    def add_panel(panel_piece):
        return jnp.dot(normed, panel_piece, preferred_element_type=jnp.float32)

    query_proj = add_panel(lax.all_gather(query_weight, "row", axis=0, tiled=True))
    projected_keys = add_panel(lax.all_gather(key_matrix, "row", axis=0, tiled=True))
    projected_values = add_panel(lax.all_gather(value_matrix, "row", axis=0, tiled=True))
    head_size = query_gain.shape[0]
    query_heads = query_weight.shape[1] // head_size
    pair_heads = key_matrix.shape[1] // head_size
    group_count = query_heads // pair_heads
    scale_factor = float(MODEL_WIDTH // QUERY_HEAD_COUNT) ** (-0.5)
    row_index = lax.axis_index("row")
    query_places = row_index * tokens + jnp.arange(tokens, dtype=jnp.int32)
    query_rot = apply_rotary(
        root_mean_scale(query_proj.reshape(tokens, query_heads, head_size), query_gain),
        query_places.astype(jnp.float32),
    ).astype(jnp.bfloat16)
    rotary_keys = apply_rotary(
        root_mean_scale(projected_keys.reshape(tokens, pair_heads, head_size), key_norm_gain),
        query_places.astype(jnp.float32),
    ).astype(jnp.bfloat16)
    keys_flat = rotary_keys.reshape(tokens, pair_heads * head_size)
    values_flat = projected_values.astype(jnp.bfloat16)
    shards_back = min(WINDOW_LENGTH // tokens, lax.axis_size("row") - 1)
    band_length = (shards_back + 1) * tokens
    key_parts = [keys_flat]
    value_parts = [values_flat]
    for offset in range(1, shards_back + 1):
        keys_prior, values_prior = shifted((keys_flat, values_flat), "row", offset)
        key_parts = [keys_prior] + key_parts
        value_parts = [values_prior] + value_parts
    keys_band = jnp.concatenate(key_parts, axis=0)
    values_band = jnp.concatenate(value_parts, axis=0)
    key_places = (row_index - shards_back) * tokens + jnp.arange(band_length, dtype=jnp.int32)
    distance = query_places[:, None] - key_places[None, :]
    visible = (distance >= 0) & (distance < WINDOW_LENGTH) & (key_places[None, :] >= 0)
    grouped = query_rot.reshape(tokens, pair_heads, group_count, head_size)
    scores = (
        jnp.einsum(
            "qhgd,shd->hgqs",
            grouped,
            keys_band.reshape(band_length, pair_heads, head_size),
            preferred_element_type=jnp.float32,
        )
        * scale_factor
    )
    scores = jnp.where(visible, scores, -1e30)
    row_max = jnp.max(scores, axis=-1, keepdims=True)
    exponent = jnp.exp(scores - row_max)
    weights = (exponent / jnp.sum(exponent, axis=-1, keepdims=True)).astype(jnp.bfloat16)
    attended = jnp.einsum(
        "hgqs,shd->qhgd",
        weights,
        values_band.reshape(band_length, pair_heads, head_size),
        preferred_element_type=jnp.float32,
    )
    heads_out = attended.reshape(tokens, query_heads * head_size).astype(jnp.bfloat16)
    head_rows = lax.all_gather(heads_out, ("col", "sub"), axis=1, tiled=True)
    branch = jnp.dot(
        head_rows,
        lax.all_gather(output_weight, "row", axis=0, tiled=True),
        preferred_element_type=jnp.float32,
    )
    squares = lax.psum(jnp.sum(branch * branch, axis=-1), ("col", "sub"))
    scaled = branch * lax.rsqrt(squares[:, None] / MODEL_WIDTH + EPSILON) * post_gain
    return (stream_in.astype(jnp.float32) + scaled).astype(jnp.bfloat16)


def swapped(x):
    count = lax.axis_size("groups")
    return lax.ppermute(x, "groups", [(i, count - 1 - i) for i in range(count)])


def rows_gathered(piece):
    return lax.all_gather(piece, "row", axis=0)


def attend(query_rot, keys_flat, values_flat, row_index, head_size, scale_factor):
    tokens, kv_width = keys_flat.shape
    pair_heads = kv_width // head_size
    group_count = query_rot.shape[1] // pair_heads
    query_places = row_index * tokens + jnp.arange(tokens, dtype=jnp.int32)
    shards_back = min(WINDOW_LENGTH // tokens, lax.axis_size("row") - 1)
    band_length = (shards_back + 1) * tokens
    key_parts = [keys_flat]
    value_parts = [values_flat]
    for offset in range(1, shards_back + 1):
        keys_prior, values_prior = shifted((keys_flat, values_flat), "row", offset)
        key_parts = [keys_prior] + key_parts
        value_parts = [values_prior] + value_parts
    keys_band = jnp.concatenate(key_parts, axis=0)
    values_band = jnp.concatenate(value_parts, axis=0)
    key_places = (row_index - shards_back) * tokens + jnp.arange(band_length, dtype=jnp.int32)
    distance = query_places[:, None] - key_places[None, :]
    visible = (distance >= 0) & (distance < WINDOW_LENGTH) & (key_places[None, :] >= 0)
    grouped = query_rot.reshape(tokens, pair_heads, group_count, head_size)
    scores = (
        jnp.einsum(
            "qhgd,shd->hgqs",
            grouped,
            keys_band.reshape(band_length, pair_heads, head_size),
            preferred_element_type=jnp.float32,
        )
        * scale_factor
    )
    scores = jnp.where(visible, scores, -1e30)
    row_max = jnp.max(scores, axis=-1, keepdims=True)
    exponent = jnp.exp(scores - row_max)
    weights = (exponent / jnp.sum(exponent, axis=-1, keepdims=True)).astype(jnp.bfloat16)
    attended = jnp.einsum(
        "hgqs,shd->qhgd",
        weights,
        values_band.reshape(band_length, pair_heads, head_size),
        preferred_element_type=jnp.float32,
    )
    return attended.reshape(tokens, -1).astype(jnp.bfloat16)


def on_device_sharing(
    stream_in,
    in_gain,
    query_weight,
    key_matrix,
    value_matrix,
    query_gain,
    key_norm_gain,
    output_weight,
    post_gain,
):
    group = lax.axis_index("groups")
    head_size = query_gain.shape[0]
    rows = lax.axis_size("row")

    def own_columns(w):
        width = w.shape[1] // 2
        return lax.dynamic_slice_in_dim(w, group * width, width, axis=1)

    def halves(w):
        own = rows_gathered(own_columns(w))
        other = swapped(own)
        full = rows * w.shape[0]
        return own.reshape(full, -1), other.reshape(full, -1)

    key_halves = halves(key_matrix)
    token_rows = lax.all_gather(stream_in, ("col", "sub"), axis=1, tiled=True)
    value_halves = halves(value_matrix)
    query_halves = halves(query_weight)
    depth = output_weight.shape[0]
    half, quarter = depth // 2, depth // 4
    out_own = rows_gathered(lax.dynamic_slice_in_dim(output_weight, group * half, half, axis=0))
    out_peer = swapped(out_own[:, :quarter])
    out_direct = rows_gathered(
        lax.dynamic_slice_in_dim(output_weight, (1 - group) * half + quarter, quarter, axis=0)
    )

    tokens = token_rows.shape[0]
    normed = root_mean_scale(token_rows.astype(jnp.float32), in_gain).astype(jnp.bfloat16)

    def add_panel(panel):
        return jnp.dot(normed, panel, preferred_element_type=jnp.float32)

    scale_factor = float(MODEL_WIDTH // QUERY_HEAD_COUNT) ** (-0.5)
    row_index = lax.axis_index("row")
    places = (row_index * tokens + jnp.arange(tokens, dtype=jnp.int32)).astype(jnp.float32)

    def rotated(projected, gain):
        heads = projected.reshape(tokens, -1, head_size)
        return apply_rotary(root_mean_scale(heads, gain), places).astype(jnp.bfloat16)

    attended = []
    for i in range(2):
        keys_flat = rotated(add_panel(key_halves[i]), key_norm_gain).reshape(tokens, -1)
        values_flat = add_panel(value_halves[i]).astype(jnp.bfloat16)
        query_rot = rotated(add_panel(query_halves[i]), query_gain)
        heads_out = attend(query_rot, keys_flat, values_flat, row_index, head_size, scale_factor)
        attended.append(lax.all_gather(heads_out, ("col", "sub"), axis=1, tiled=True))
    own_rows, other_rows = attended
    blocks = other_rows.reshape(tokens, -1, half)
    branch = (
        jnp.dot(own_rows, out_own.reshape(-1, out_own.shape[-1]), preferred_element_type=jnp.float32)
        + jnp.dot(
            blocks[:, :, quarter:].reshape(tokens, -1),
            out_direct.reshape(-1, out_direct.shape[-1]),
            preferred_element_type=jnp.float32,
        )
        + jnp.dot(
            blocks[:, :, :quarter].reshape(tokens, -1),
            out_peer.reshape(-1, out_peer.shape[-1]),
            preferred_element_type=jnp.float32,
        )
    )
    squares = lax.psum(jnp.sum(branch * branch, axis=-1), ("col", "sub"))
    scaled = branch * lax.rsqrt(squares[:, None] / MODEL_WIDTH + EPSILON) * post_gain
    return (stream_in.astype(jnp.float32) + scaled).astype(jnp.bfloat16)


def on_device_any(*operands):
    head_size = operands[5].shape[0]
    pair_heads = operands[3].shape[1] // head_size
    blocks_agree = lax.axis_size("row") == lax.axis_size("col") * lax.axis_size("sub")
    if lax.axis_size("groups") == 2 and pair_heads % 2 == 0 and blocks_agree:
        return on_device_sharing(*operands)
    return on_device(*operands)


def solution(mesh):
    placed = (
        P(("groups", "row"), ("col", "sub")),
        P(),
        P("row", ("col", "sub")),
        P("row", ("col", "sub")),
        P("row", ("col", "sub")),
        P(),
        P(),
        P("row", ("col", "sub")),
        P(("col", "sub")),
    )
    return jax.shard_map(
        on_device_any,
        mesh=mesh,
        in_specs=placed,
        out_specs=P(("groups", "row"), ("col", "sub")),
        check_vma=False,
    )
```

```python
import jax
import jax.numpy as jnp
from jax import lax
from jax.sharding import PartitionSpec as P

MODEL_WIDTH = 5376
QUERY_HEAD_COUNT = 32
WINDOW_LENGTH = 1024


EPSILON = 1e-06


def shifted(x, axis, by):
    count = lax.axis_size(axis)
    pairs = [(i, i + by) for i in range(count) if 0 <= i + by < count]
    return lax.ppermute(x, axis, pairs)


def root_mean_scale(values, gain):
    return values * lax.rsqrt(jnp.mean(values * values, axis=-1, keepdims=True) + EPSILON) * gain


def apply_rotary(tensor, token_positions):
    half_dim = tensor.shape[-1] // 2
    inverse = 10000.0 ** (-(jnp.arange(half_dim, dtype=jnp.float32) * 2.0) / tensor.shape[-1])
    angles = token_positions[:, None] * inverse[None, :]
    cosine = jnp.cos(angles)[:, None, :]
    sine_part = jnp.sin(angles)[:, None, :]
    first_half = tensor[..., :half_dim]
    second_half = tensor[..., half_dim:]
    return jnp.concatenate(
        [
            first_half * cosine - second_half * sine_part,
            second_half * cosine + first_half * sine_part,
        ],
        axis=-1,
    )


def on_device(
    stream_in,
    in_gain,
    query_weight,
    key_matrix,
    value_matrix,
    query_gain,
    key_norm_gain,
    output_weight,
    post_gain,
):
    token_rows = lax.all_gather(stream_in, ("col", "sub"), axis=1, tiled=True)
    tokens = token_rows.shape[0]
    normed = root_mean_scale(token_rows.astype(jnp.float32), in_gain).astype(jnp.bfloat16)

    def add_panel(panel_piece):
        return jnp.dot(normed, panel_piece, preferred_element_type=jnp.float32)

    query_proj = add_panel(lax.all_gather(query_weight, "row", axis=0, tiled=True))
    projected_keys = add_panel(lax.all_gather(key_matrix, "row", axis=0, tiled=True))
    projected_values = add_panel(lax.all_gather(value_matrix, "row", axis=0, tiled=True))
    head_size = query_gain.shape[0]
    query_heads = query_weight.shape[1] // head_size
    pair_heads = key_matrix.shape[1] // head_size
    group_count = query_heads // pair_heads
    scale_factor = float(MODEL_WIDTH // QUERY_HEAD_COUNT) ** (-0.5)
    row_index = lax.axis_index("row")
    query_places = row_index * tokens + jnp.arange(tokens, dtype=jnp.int32)
    query_rot = apply_rotary(
        root_mean_scale(query_proj.reshape(tokens, query_heads, head_size), query_gain),
        query_places.astype(jnp.float32),
    ).astype(jnp.bfloat16)
    rotary_keys = apply_rotary(
        root_mean_scale(projected_keys.reshape(tokens, pair_heads, head_size), key_norm_gain),
        query_places.astype(jnp.float32),
    ).astype(jnp.bfloat16)
    keys_flat = rotary_keys.reshape(tokens, pair_heads * head_size)
    values_flat = projected_values.astype(jnp.bfloat16)
    shards_back = min(WINDOW_LENGTH // tokens, lax.axis_size("row") - 1)
    band_length = (shards_back + 1) * tokens
    key_parts = [keys_flat]
    value_parts = [values_flat]
    for offset in range(1, shards_back + 1):
        keys_prior, values_prior = shifted((keys_flat, values_flat), "row", offset)
        key_parts = [keys_prior] + key_parts
        value_parts = [values_prior] + value_parts
    keys_band = jnp.concatenate(key_parts, axis=0)
    values_band = jnp.concatenate(value_parts, axis=0)
    key_places = (row_index - shards_back) * tokens + jnp.arange(band_length, dtype=jnp.int32)
    distance = query_places[:, None] - key_places[None, :]
    visible = (distance >= 0) & (distance < WINDOW_LENGTH) & (key_places[None, :] >= 0)
    grouped = query_rot.reshape(tokens, pair_heads, group_count, head_size)
    scores = (
        jnp.einsum(
            "qhgd,shd->hgqs",
            grouped,
            keys_band.reshape(band_length, pair_heads, head_size),
            preferred_element_type=jnp.float32,
        )
        * scale_factor
    )
    scores = jnp.where(visible, scores, -1e30)
    row_max = jnp.max(scores, axis=-1, keepdims=True)
    exponent = jnp.exp(scores - row_max)
    weights = (exponent / jnp.sum(exponent, axis=-1, keepdims=True)).astype(jnp.bfloat16)
    attended = jnp.einsum(
        "hgqs,shd->qhgd",
        weights,
        values_band.reshape(band_length, pair_heads, head_size),
        preferred_element_type=jnp.float32,
    )
    heads_out = attended.reshape(tokens, query_heads * head_size).astype(jnp.bfloat16)
    head_rows = lax.all_gather(heads_out, ("col", "sub"), axis=1, tiled=True)
    branch = jnp.dot(
        head_rows,
        lax.all_gather(output_weight, "row", axis=0, tiled=True),
        preferred_element_type=jnp.float32,
    )
    squares = lax.psum(jnp.sum(branch * branch, axis=-1), ("col", "sub"))
    scaled = branch * lax.rsqrt(squares[:, None] / MODEL_WIDTH + EPSILON) * post_gain
    return (stream_in.astype(jnp.float32) + scaled).astype(jnp.bfloat16)


def swapped(x):
    count = lax.axis_size("groups")
    return lax.ppermute(x, "groups", [(i, count - 1 - i) for i in range(count)])


def ring_next(x):
    count = lax.axis_size("row")
    return lax.ppermute(x, "row", [(i, (i + 1) % count) for i in range(count)])


def ring_blocks(own, other):
    blocks = [(own, other)]
    for step in range(1, lax.axis_size("row")):
        own, other = blocks[-1]
        if step > 2:
            earlier_own, earlier = blocks[-2]
            own, earlier = lax.optimization_barrier((own, earlier))
            blocks[-2] = (earlier_own, earlier)
            blocks[-1] = (own, other)
        own = ring_next(own)
        blocks.append((own, swapped(own)))
    return blocks


def attend(query_rot, keys_flat, values_flat, row_index, head_size, scale_factor):
    tokens, kv_width = keys_flat.shape
    pair_heads = kv_width // head_size
    group_count = query_rot.shape[1] // pair_heads
    query_places = row_index * tokens + jnp.arange(tokens, dtype=jnp.int32)
    shards_back = min(WINDOW_LENGTH // tokens, lax.axis_size("row") - 1)
    band_length = (shards_back + 1) * tokens
    key_parts = [keys_flat]
    value_parts = [values_flat]
    for offset in range(1, shards_back + 1):
        keys_prior, values_prior = shifted((keys_flat, values_flat), "row", offset)
        key_parts = [keys_prior] + key_parts
        value_parts = [values_prior] + value_parts
    keys_band = jnp.concatenate(key_parts, axis=0)
    values_band = jnp.concatenate(value_parts, axis=0)
    key_places = (row_index - shards_back) * tokens + jnp.arange(band_length, dtype=jnp.int32)
    distance = query_places[:, None] - key_places[None, :]
    visible = (distance >= 0) & (distance < WINDOW_LENGTH) & (key_places[None, :] >= 0)
    grouped = query_rot.reshape(tokens, pair_heads, group_count, head_size)
    scores = (
        jnp.einsum(
            "qhgd,shd->hgqs",
            grouped,
            keys_band.reshape(band_length, pair_heads, head_size),
            preferred_element_type=jnp.float32,
        )
        * scale_factor
    )
    scores = jnp.where(visible, scores, -1e30)
    row_max = jnp.max(scores, axis=-1, keepdims=True)
    exponent = jnp.exp(scores - row_max)
    weights = (exponent / jnp.sum(exponent, axis=-1, keepdims=True)).astype(jnp.bfloat16)
    attended = jnp.einsum(
        "hgqs,shd->qhgd",
        weights,
        values_band.reshape(band_length, pair_heads, head_size),
        preferred_element_type=jnp.float32,
    )
    return attended.reshape(tokens, -1).astype(jnp.bfloat16)


def on_device_sharing(
    stream_in,
    in_gain,
    query_weight,
    key_matrix,
    value_matrix,
    query_gain,
    key_norm_gain,
    output_weight,
    post_gain,
):
    group = lax.axis_index("groups")
    head_size = query_gain.shape[0]
    rows = lax.axis_size("row")

    row_index = lax.axis_index("row")

    def side(w, which, axis):
        size = w.shape[axis] // 2
        return lax.dynamic_slice_in_dim(w, which * size, size, axis=axis)

    def both(operands, axis):
        return [
            jnp.concatenate([side(w, which, axis) for w in operands], axis=1)
            for which in (group, 1 - group)
        ]

    token_rows = lax.all_gather(stream_in, ("col", "sub"), axis=1, tiled=True)
    pair_blocks = ring_blocks(*both([key_matrix, value_matrix], 1))
    query_blocks = ring_blocks(*both([query_weight], 1))
    out_sides = both([output_weight], 0)
    query_own, out_sides[0] = lax.optimization_barrier((query_blocks[2][0], out_sides[0]))
    query_blocks[2] = (query_own, query_blocks[2][1])
    first_hop = ring_next(out_sides[0])
    out_blocks = [tuple(out_sides), (first_hop, swapped(first_hop))]

    def send_out(value):
        own, other = out_blocks[-1]
        value, own = lax.optimization_barrier((value, own))
        out_blocks[-1] = (own, other)
        own = ring_next(own)
        out_blocks.append((own, swapped(own)))
        return value


    tokens = token_rows.shape[0]
    normed = root_mean_scale(token_rows.astype(jnp.float32), in_gain).astype(jnp.bfloat16)

    def picked(whole, step):
        width = whole.shape[1] // rows
        place = lax.rem(row_index - step + rows, rows)
        return lax.dynamic_slice_in_dim(whole, place * width, width, axis=1)

    def summed(whole, blocks, which):
        return sum(
            jnp.dot(picked(whole, step), pair[which], preferred_element_type=jnp.float32)
            for step, pair in enumerate(blocks)
        )

    scale_factor = float(MODEL_WIDTH // QUERY_HEAD_COUNT) ** (-0.5)
    places = (row_index * tokens + jnp.arange(tokens, dtype=jnp.int32)).astype(jnp.float32)

    def rotated(projected, gain):
        heads = projected.reshape(tokens, -1, head_size)
        return apply_rotary(root_mean_scale(heads, gain), places).astype(jnp.bfloat16)

    attended = []
    for i in range(2):
        pair = summed(normed, pair_blocks, i)
        width = pair.shape[1] // 2
        keys_flat = rotated(pair[:, :width], key_norm_gain).reshape(tokens, -1)
        values_flat = pair[:, width:].astype(jnp.bfloat16)
        query_rot = rotated(summed(normed, query_blocks, i), query_gain)
        if i == 0:
            query_rot = send_out(query_rot)
        else:
            query_rot, out_blocks[1:-1], last_own = lax.optimization_barrier(
                (query_rot, out_blocks[1:-1], out_blocks[-1][0])
            )
            out_blocks[-1] = (last_own, out_blocks[-1][1])
        heads_out = attend(query_rot, keys_flat, values_flat, row_index, head_size, scale_factor)
        if i == 1:
            heads_out, out_blocks[-1] = lax.optimization_barrier((heads_out, out_blocks[-1]))
        while i == 0 and len(out_blocks) < rows:
            heads_out = send_out(heads_out)
        attended.append(lax.all_gather(heads_out, ("col", "sub"), axis=1, tiled=True))
    branch = summed(attended[0], out_blocks, 0) + summed(attended[1], out_blocks, 1)
    squares = lax.psum(jnp.sum(branch * branch, axis=-1), ("col", "sub"))
    scaled = branch * lax.rsqrt(squares[:, None] / MODEL_WIDTH + EPSILON) * post_gain
    return (stream_in.astype(jnp.float32) + scaled).astype(jnp.bfloat16)


def on_device_any(*operands):
    head_size = operands[5].shape[0]
    pair_heads = operands[3].shape[1] // head_size
    blocks_agree = lax.axis_size("row") == lax.axis_size("col") * lax.axis_size("sub")
    long_enough = lax.axis_size("row") > 2
    if lax.axis_size("groups") == 2 and pair_heads % 2 == 0 and blocks_agree and long_enough:
        return on_device_sharing(*operands)
    return on_device(*operands)


def solution(mesh):
    placed = (
        P(("groups", "row"), ("col", "sub")),
        P(),
        P("row", ("col", "sub")),
        P("row", ("col", "sub")),
        P("row", ("col", "sub")),
        P(),
        P(),
        P("row", ("col", "sub")),
        P(("col", "sub")),
    )
    return jax.shard_map(
        on_device_any,
        mesh=mesh,
        in_specs=placed,
        out_specs=P(("groups", "row"), ("col", "sub")),
        check_vma=False,
    )
```

```python
import jax
import jax.numpy as jnp
from jax import lax
from jax.sharding import PartitionSpec as P

MODEL_WIDTH = 5376
QUERY_HEAD_COUNT = 32
WINDOW_LENGTH = 1024


EPSILON = 1e-06


def shifted(x, axis, by):
    count = lax.axis_size(axis)
    pairs = [(i, i + by) for i in range(count) if 0 <= i + by < count]
    return lax.ppermute(x, axis, pairs)


def root_mean_scale(values, gain):
    return values * lax.rsqrt(jnp.mean(values * values, axis=-1, keepdims=True) + EPSILON) * gain


def apply_rotary(tensor, token_positions):
    half_dim = tensor.shape[-1] // 2
    inverse = 10000.0 ** (-(jnp.arange(half_dim, dtype=jnp.float32) * 2.0) / tensor.shape[-1])
    angles = token_positions[:, None] * inverse[None, :]
    cosine = jnp.cos(angles)[:, None, :]
    sine_part = jnp.sin(angles)[:, None, :]
    first_half = tensor[..., :half_dim]
    second_half = tensor[..., half_dim:]
    return jnp.concatenate(
        [
            first_half * cosine - second_half * sine_part,
            second_half * cosine + first_half * sine_part,
        ],
        axis=-1,
    )


def on_device(
    stream_in,
    in_gain,
    query_weight,
    key_matrix,
    value_matrix,
    query_gain,
    key_norm_gain,
    output_weight,
    post_gain,
):
    token_rows = lax.all_gather(stream_in, ("col", "sub"), axis=1, tiled=True)
    tokens = token_rows.shape[0]
    normed = root_mean_scale(token_rows.astype(jnp.float32), in_gain).astype(jnp.bfloat16)

    def add_panel(panel_piece):
        return jnp.dot(normed, panel_piece, preferred_element_type=jnp.float32)

    query_proj = add_panel(lax.all_gather(query_weight, "row", axis=0, tiled=True))
    projected_keys = add_panel(lax.all_gather(key_matrix, "row", axis=0, tiled=True))
    projected_values = add_panel(lax.all_gather(value_matrix, "row", axis=0, tiled=True))
    head_size = query_gain.shape[0]
    query_heads = query_weight.shape[1] // head_size
    pair_heads = key_matrix.shape[1] // head_size
    group_count = query_heads // pair_heads
    scale_factor = float(MODEL_WIDTH // QUERY_HEAD_COUNT) ** (-0.5)
    row_index = lax.axis_index("row")
    query_places = row_index * tokens + jnp.arange(tokens, dtype=jnp.int32)
    query_rot = apply_rotary(
        root_mean_scale(query_proj.reshape(tokens, query_heads, head_size), query_gain),
        query_places.astype(jnp.float32),
    ).astype(jnp.bfloat16)
    rotary_keys = apply_rotary(
        root_mean_scale(projected_keys.reshape(tokens, pair_heads, head_size), key_norm_gain),
        query_places.astype(jnp.float32),
    ).astype(jnp.bfloat16)
    keys_flat = rotary_keys.reshape(tokens, pair_heads * head_size)
    values_flat = projected_values.astype(jnp.bfloat16)
    shards_back = min(WINDOW_LENGTH // tokens, lax.axis_size("row") - 1)
    band_length = (shards_back + 1) * tokens
    key_parts = [keys_flat]
    value_parts = [values_flat]
    for offset in range(1, shards_back + 1):
        keys_prior, values_prior = shifted((keys_flat, values_flat), "row", offset)
        key_parts = [keys_prior] + key_parts
        value_parts = [values_prior] + value_parts
    keys_band = jnp.concatenate(key_parts, axis=0)
    values_band = jnp.concatenate(value_parts, axis=0)
    key_places = (row_index - shards_back) * tokens + jnp.arange(band_length, dtype=jnp.int32)
    distance = query_places[:, None] - key_places[None, :]
    visible = (distance >= 0) & (distance < WINDOW_LENGTH) & (key_places[None, :] >= 0)
    grouped = query_rot.reshape(tokens, pair_heads, group_count, head_size)
    scores = (
        jnp.einsum(
            "qhgd,shd->hgqs",
            grouped,
            keys_band.reshape(band_length, pair_heads, head_size),
            preferred_element_type=jnp.float32,
        )
        * scale_factor
    )
    scores = jnp.where(visible, scores, -1e30)
    row_max = jnp.max(scores, axis=-1, keepdims=True)
    exponent = jnp.exp(scores - row_max)
    weights = (exponent / jnp.sum(exponent, axis=-1, keepdims=True)).astype(jnp.bfloat16)
    attended = jnp.einsum(
        "hgqs,shd->qhgd",
        weights,
        values_band.reshape(band_length, pair_heads, head_size),
        preferred_element_type=jnp.float32,
    )
    heads_out = attended.reshape(tokens, query_heads * head_size).astype(jnp.bfloat16)
    head_rows = lax.all_gather(heads_out, ("col", "sub"), axis=1, tiled=True)
    branch = jnp.dot(
        head_rows,
        lax.all_gather(output_weight, "row", axis=0, tiled=True),
        preferred_element_type=jnp.float32,
    )
    squares = lax.psum(jnp.sum(branch * branch, axis=-1), ("col", "sub"))
    scaled = branch * lax.rsqrt(squares[:, None] / MODEL_WIDTH + EPSILON) * post_gain
    return (stream_in.astype(jnp.float32) + scaled).astype(jnp.bfloat16)


def swapped(x):
    count = lax.axis_size("groups")
    return lax.ppermute(x, "groups", [(i, count - 1 - i) for i in range(count)])


def ring_next(x):
    count = lax.axis_size("row")
    return lax.ppermute(x, "row", [(i, (i + 1) % count) for i in range(count)])


def ring_blocks(own, other):
    blocks = [(own, other)]
    for step in range(1, lax.axis_size("row")):
        own, other = blocks[-1]
        if step > 2:
            earlier_own, earlier = blocks[-2]
            own, earlier = lax.optimization_barrier((own, earlier))
            blocks[-2] = (earlier_own, earlier)
            blocks[-1] = (own, other)
        own = ring_next(own)
        blocks.append((own, swapped(own)))
    return blocks


def banded(keys_flat, values_flat):
    shards_back = min(WINDOW_LENGTH // keys_flat.shape[0], lax.axis_size("row") - 1)
    key_parts = [keys_flat]
    value_parts = [values_flat]
    for offset in range(1, shards_back + 1):
        keys_prior, values_prior = shifted((keys_flat, values_flat), "row", offset)
        key_parts = [keys_prior] + key_parts
        value_parts = [values_prior] + value_parts
    return key_parts, value_parts


def attend(query_rot, key_parts, value_parts, row_index, head_size, scale_factor):
    tokens, kv_width = key_parts[0].shape
    pair_heads = kv_width // head_size
    group_count = query_rot.shape[1] // pair_heads
    query_places = row_index * tokens + jnp.arange(tokens, dtype=jnp.int32)
    shards_back = len(key_parts) - 1
    band_length = (shards_back + 1) * tokens
    keys_band = jnp.concatenate(key_parts, axis=0)
    values_band = jnp.concatenate(value_parts, axis=0)
    key_places = (row_index - shards_back) * tokens + jnp.arange(band_length, dtype=jnp.int32)
    distance = query_places[:, None] - key_places[None, :]
    visible = (distance >= 0) & (distance < WINDOW_LENGTH) & (key_places[None, :] >= 0)
    grouped = query_rot.reshape(tokens, pair_heads, group_count, head_size)
    scores = (
        jnp.einsum(
            "qhgd,shd->hgqs",
            grouped,
            keys_band.reshape(band_length, pair_heads, head_size),
            preferred_element_type=jnp.float32,
        )
        * scale_factor
    )
    scores = jnp.where(visible, scores, -1e30)
    row_max = jnp.max(scores, axis=-1, keepdims=True)
    exponent = jnp.exp(scores - row_max)
    weights = (exponent / jnp.sum(exponent, axis=-1, keepdims=True)).astype(jnp.bfloat16)
    attended = jnp.einsum(
        "hgqs,shd->qhgd",
        weights,
        values_band.reshape(band_length, pair_heads, head_size),
        preferred_element_type=jnp.float32,
    )
    return attended.reshape(tokens, -1).astype(jnp.bfloat16)


def on_device_sharing(
    stream_in,
    in_gain,
    query_weight,
    key_matrix,
    value_matrix,
    query_gain,
    key_norm_gain,
    output_weight,
    post_gain,
):
    group = lax.axis_index("groups")
    head_size = query_gain.shape[0]
    rows = lax.axis_size("row")

    row_index = lax.axis_index("row")

    def side(w, which, axis):
        size = w.shape[axis] // 2
        return lax.dynamic_slice_in_dim(w, which * size, size, axis=axis)

    def both(operands, axis):
        return [
            jnp.concatenate([side(w, which, axis) for w in operands], axis=1)
            for which in (group, 1 - group)
        ]

    token_rows = lax.all_gather(stream_in, ("col", "sub"), axis=1, tiled=True)
    pair_blocks = ring_blocks(*both([key_matrix, value_matrix], 1))
    query_blocks = ring_blocks(*both([query_weight], 1))
    out_sides = both([output_weight], 0)
    query_own, out_sides[0] = lax.optimization_barrier((query_blocks[2][0], out_sides[0]))
    query_blocks[2] = (query_own, query_blocks[2][1])
    first_hop = ring_next(out_sides[0])
    out_blocks = [tuple(out_sides), (first_hop, swapped(first_hop))]

    def send_out(value):
        own, other = out_blocks[-1]
        value, own = lax.optimization_barrier((value, own))
        out_blocks[-1] = (own, other)
        own = ring_next(own)
        out_blocks.append((own, swapped(own)))
        return value


    tokens = token_rows.shape[0]
    normed = root_mean_scale(token_rows.astype(jnp.float32), in_gain).astype(jnp.bfloat16)

    def picked(whole, step):
        width = whole.shape[1] // rows
        place = lax.rem(row_index - step + rows, rows)
        return lax.dynamic_slice_in_dim(whole, place * width, width, axis=1)

    def summed(whole, blocks, which):
        return sum(
            jnp.dot(picked(whole, step), pair[which], preferred_element_type=jnp.float32)
            for step, pair in enumerate(blocks)
        )

    scale_factor = float(MODEL_WIDTH // QUERY_HEAD_COUNT) ** (-0.5)
    places = (row_index * tokens + jnp.arange(tokens, dtype=jnp.int32)).astype(jnp.float32)

    def rotated(projected, gain):
        heads = projected.reshape(tokens, -1, head_size)
        return apply_rotary(root_mean_scale(heads, gain), places).astype(jnp.bfloat16)

    def keys_values(i):
        pair = summed(normed, pair_blocks, i)
        width = pair.shape[1] // 2
        keys_flat = rotated(pair[:, :width], key_norm_gain).reshape(tokens, -1)
        return keys_flat, pair[:, width:].astype(jnp.bfloat16)

    def queries(i):
        return rotated(summed(normed, query_blocks, i), query_gain)

    def gathered(heads_out):
        return lax.all_gather(heads_out, ("col", "sub"), axis=1, tiled=True)

    own_pair = send_out(keys_values(0))
    own_band = banded(*own_pair)
    own_query = queries(0)
    while len(out_blocks) < rows:
        own_query = send_out(own_query)
    own_query, other_pair = lax.optimization_barrier((own_query, keys_values(1)))
    other_band = banded(*other_pair)
    own_heads = attend(own_query, *own_band, row_index, head_size, scale_factor)
    own_heads, other_band = lax.optimization_barrier((own_heads, other_band))
    own_attended = gathered(own_heads)
    other_query, out_blocks[1:-1], last_own = lax.optimization_barrier(
        (queries(1), out_blocks[1:-1], out_blocks[-1][0])
    )
    out_blocks[-1] = (last_own, out_blocks[-1][1])
    other_heads = attend(other_query, *other_band, row_index, head_size, scale_factor)
    other_heads, out_blocks[-1] = lax.optimization_barrier((other_heads, out_blocks[-1]))
    attended = (own_attended, gathered(other_heads))
    branch = summed(attended[0], out_blocks, 0) + summed(attended[1], out_blocks, 1)
    squares = lax.psum(jnp.sum(branch * branch, axis=-1), ("col", "sub"))
    scaled = branch * lax.rsqrt(squares[:, None] / MODEL_WIDTH + EPSILON) * post_gain
    return (stream_in.astype(jnp.float32) + scaled).astype(jnp.bfloat16)


def on_device_any(*operands):
    head_size = operands[5].shape[0]
    pair_heads = operands[3].shape[1] // head_size
    blocks_agree = lax.axis_size("row") == lax.axis_size("col") * lax.axis_size("sub")
    long_enough = lax.axis_size("row") > 2
    if lax.axis_size("groups") == 2 and pair_heads % 2 == 0 and blocks_agree and long_enough:
        return on_device_sharing(*operands)
    return on_device(*operands)


def solution(mesh):
    placed = (
        P(("groups", "row"), ("col", "sub")),
        P(),
        P("row", ("col", "sub")),
        P("row", ("col", "sub")),
        P("row", ("col", "sub")),
        P(),
        P(),
        P("row", ("col", "sub")),
        P(("col", "sub")),
    )
    return jax.shard_map(
        on_device_any,
        mesh=mesh,
        in_specs=placed,
        out_specs=P(("groups", "row"), ("col", "sub")),
        check_vma=False,
    )
```
